32 devices in a mesh: dp: 8 (over z, y), mp: 4 (over x, core).
Axes of the slice: x: 2, y: 2, z: 4, core: 2. Of those that a mesh axis runs over, the one named last changes fastest.
Arguments:
- tokens: bfloat16 [16, 2048, 768], P('dp', 'mp'), may hold values from -6 to 6
- lengths: int32 [16], replicated, may hold values from 1 to 2048, as said below
- order: int32 [16], replicated, may hold values from 0 to 15, as said below
- q_weight: bfloat16 [768, 768], P(('dp', 'mp')), may hold values from -0.21875 to 0.21875
- k_weight: bfloat16 [768, 768], P(('dp', 'mp')), may hold values from -0.21875 to 0.21875
- v_weight: bfloat16 [768, 768], P(('dp', 'mp')), may hold values from -0.21875 to 0.21875
- o_weight: bfloat16 [768, 768], P(('dp', 'mp')), may hold values from -6 to 6
- q_bias: bfloat16 [768], P(('dp', 'mp')), may hold values from -1.1953125 to 1.1953125
- v_bias: bfloat16 [768], P(('dp', 'mp')), may hold values from -0.059814453 to 0.059814453
- o_bias: bfloat16 [768], P(('dp', 'mp')), may hold values from -1.1953125 to 1.1953125
- attn_gain: bfloat16 [768], P(('dp', 'mp')), may hold values from 0.5 to 1.5
- attn_shift: bfloat16 [768], P(('dp', 'mp')), may hold values from -1.1953125 to 1.1953125
- in_weight: bfloat16 [768, 3072], P(('dp', 'mp')), may hold values from -0.21875 to 0.21875
- in_bias: bfloat16 [3072], P(('dp', 'mp')), may hold values from -1.1953125 to 1.1953125
- out_weight: bfloat16 [3072, 768], P(('dp', 'mp')), may hold values from -0.109375 to 0.109375
- out_bias: bfloat16 [768], P(('dp', 'mp')), may hold values from -1.1953125 to 1.1953125
- ffn_gain: bfloat16 [768], P(('dp', 'mp')), may hold values from 0.5 to 1.5
- ffn_shift: bfloat16 [768], P(('dp', 'mp')), may hold values from -1.1953125 to 1.1953125
- cotangent: bfloat16 [16, 2048, 768], P('dp', 'mp'), may hold values from -6 to 6
Outputs:
- output: bfloat16 [16, 2048, 768], P('dp', 'mp')
- input_grad: float32 [16, 2048, 768], P('dp', 'mp')
- q_weight_grad: float32 [768, 768], P(('dp', 'mp'))
- k_weight_grad: float32 [768, 768], P(('dp', 'mp'))
- v_weight_grad: float32 [768, 768], P(('dp', 'mp'))
- o_weight_grad: float32 [768, 768], P(('dp', 'mp'))
- q_bias_grad: float32 [768], P(('dp', 'mp'))
- v_bias_grad: float32 [768], P(('dp', 'mp'))
- o_bias_grad: float32 [768], P(('dp', 'mp'))
- attn_gain_grad: float32 [768], P(('dp', 'mp'))
- attn_shift_grad: float32 [768], P(('dp', 'mp'))
- in_weight_grad: float32 [768, 3072], P(('dp', 'mp'))
- in_bias_grad: float32 [3072], P(('dp', 'mp'))
- out_weight_grad: float32 [3072, 768], P(('dp', 'mp'))
- out_bias_grad: float32 [768], P(('dp', 'mp'))
- ffn_gain_grad: float32 [768], P(('dp', 'mp'))
- ffn_shift_grad: float32 [768], P(('dp', 'mp'))
The draws below stay inside these ranges and needn't reach their ends.
Inputs may be any that keep to these rules, and one draw needn't show every extreme that they name: `lengths`: some sequence has exactly 2048 live positions. `order`: A permutation of the 16 sequences.
All inputs are finite; a program needn't handle non-finite values.
Results may differ from the reference program's by a relative error of at most 0.018.
Values may be sent and summed in bfloat16 or wider, within the bound.
A program may use at most 192 MiB of HBM per device.

```python
import jax
import jax.numpy as jnp
from jax import lax

D = 768
H = 12
HD = 64
FF = 3072
LEN = 2048
MICRO = 2
SEQS = 16


def deal_tables(key):
    base = jax.random.fold_in(key, 7)
    drawn = jax.random.randint(jax.random.fold_in(base, 1), (SEQS,), LEN // 8, LEN + 1, dtype=jnp.int32)
    longest = jax.random.randint(jax.random.fold_in(base, 2), (), 0, SEQS, dtype=jnp.int32)
    positions = jnp.arange(SEQS, dtype=jnp.int32)
    lengths = jnp.where(positions == longest, jnp.int32(LEN), drawn).astype(jnp.int32)
    scores = lengths * SEQS + positions
    ranked = jnp.argsort(-scores, stable=True).astype(jnp.int32)
    groups = SEQS // MICRO
    rounds = positions // groups
    within = positions % groups
    snaked = jnp.where(rounds % 2 == 0, within, groups - 1 - within)
    relabel = jax.random.permutation(jax.random.fold_in(base, 3), groups).astype(jnp.int32)
    target = relabel[snaked] * MICRO + rounds
    order = jnp.zeros((SEQS,), jnp.int32).at[target].set(ranked)
    return (lengths, order)


def draw_lengths(key, part):
    return deal_tables(key)[0]


def draw_order(key, part):
    return deal_tables(key)[1]


def with_spikes(entries, stream_key, source, target, blocks, factor):
    def block_of(position):
        return (jnp.arange(entries.shape[position]) // (entries.shape[position] // blocks)).reshape((-1,) + (1,) * (entries.ndim - 1 - position))

    near = jax.random.permutation(stream_key, blocks)[block_of(target)]
    far = (block_of(target) + blocks // 2) % blocks
    return jnp.where((block_of(source) == near) | (block_of(source) == far), factor * entries, entries)


def levels(rng, dims, shards, low, top_value):
    def one(axis_at, blocks):
        steps = jax.random.uniform(jax.random.fold_in(jax.random.fold_in(rng, 6), axis_at), (blocks,), jnp.float32, low / len(shards), top_value / len(shards))
        return jnp.repeat(jnp.exp(steps), dims[axis_at] // blocks).reshape((-1,) + (1,) * (len(dims) - axis_at - 1))

    level = one(*shards[0])
    for cut in shards[1:]:
        level = level * one(*cut)
    return level


def bell_draw(rng, extent, spread, most, cuts=(), kind=jnp.bfloat16):
    array = jax.random.normal(rng, extent, jnp.float32) * spread
    if len(cuts) > 0:
        array = levels(rng, extent, cuts, -0.22, 0.18) * array
    return jnp.clip(array, min=-most, max=most).astype(kind)


def heavy_noise(rng, dims, spread, bound, cuts, heavy, kind=jnp.bfloat16):
    entries = spread * jax.random.normal(rng, dims, jnp.float32)
    if cuts:
        entries = entries * levels(rng, dims, cuts, -0.22, 0.18)
    return jnp.clip(with_spikes(entries, jax.random.fold_in(rng, 3), *heavy), -bound, bound).astype(kind)


def setup_inputs(seed: int = 0) -> dict:
    streams_of = jax.random.split(jax.random.key(seed), 20)
    return {
        "tokens": bell_draw(streams_of[0], (SEQS, LEN, D), 1.0, 6.0, ((0, 8), (1, 4))),
        "lengths": draw_lengths(jax.random.fold_in(streams_of[19], 71), 0),
        "order": draw_order(jax.random.fold_in(streams_of[19], 71), 0),
        "q_weight": bell_draw(streams_of[3], (D, D), D ** -0.5, 0.21875, ((0, 32),)),
        "k_weight": bell_draw(streams_of[4], (D, D), D ** -0.5, 0.21875, ((0, 32),)),
        "v_weight": bell_draw(streams_of[5], (D, D), D ** -0.5, 0.21875, ((0, 32),)),
        "o_weight": bell_draw(streams_of[6], (D, D), 1 ** -0.5, 6.0, ((0, 32),)),
        "q_bias": bell_draw(streams_of[7], (D,), 0.2, 1.1953125, ((0, 32),)),
        "v_bias": bell_draw(streams_of[8], (D,), 0.01, 0.059814453, ((0, 32),)),
        "o_bias": bell_draw(streams_of[9], (D,), 0.2, 1.1953125, ((0, 32),)),
        "attn_gain": jnp.clip(1.0 + 0.1 * jax.random.normal(streams_of[10], (D,), jnp.float32), 0.5, 1.5).astype(jnp.bfloat16),
        "attn_shift": bell_draw(streams_of[11], (D,), 0.2, 1.1953125, ((0, 32),)),
        "in_weight": bell_draw(streams_of[12], (D, FF), D ** -0.5, 0.21875, ((0, 32),)),
        "in_bias": bell_draw(streams_of[13], (FF,), 0.2, 1.1953125, ((0, 32),)),
        "out_weight": bell_draw(streams_of[14], (FF, D), FF ** -0.5, 0.109375, ((0, 32),)),
        "out_bias": bell_draw(streams_of[15], (D,), 0.2, 1.1953125, ((0, 32),)),
        "ffn_gain": jnp.clip(1.0 + 0.1 * jax.random.normal(streams_of[16], (D,), jnp.float32), 0.5, 1.5).astype(jnp.bfloat16),
        "ffn_shift": bell_draw(streams_of[17], (D,), 0.2, 1.1953125, ((0, 32),)),
        "cotangent": heavy_noise(streams_of[18], (SEQS, LEN, D), 1.0, 6.0, ((0, 8), (1, 4)), (0, 2, 8, 2.0)),
    }


@jax.custom_vjp
def low(v):
    return lax.optimization_barrier(v.astype(jnp.bfloat16)).astype(jnp.float32)

@jax.custom_vjp
def low_back(v):
    return v

def low_keep(v):
    return (low(v), None)

def low_pass(kept, grad):
    return (grad,)

def back_keep(v):
    return (v, None)

def back_low(kept, grad):
    return (low(grad),)
low.defvjp(low_keep, low_pass)
low_back.defvjp(back_keep, back_low)
epsilon = 1e-05

def matmul(left, right):
    return jnp.dot(left, right, precision=lax.Precision.HIGHEST)

def layer_norm(values, gain, shift):
    center = lax.optimization_barrier(jnp.mean(values, axis=-1, keepdims=True))
    offset = values - center
    variance = lax.optimization_barrier(jnp.mean(offset * offset, axis=-1, keepdims=True))
    return offset * lax.rsqrt(variance + epsilon) * gain + shift

def forward(params, inputs, length):
    q_weight, k_weight, v_weight, o_weight, q_bias, v_bias, o_bias, attn_gain, attn_shift, in_weight, in_bias, out_weight, out_bias, ffn_gain, ffn_shift = params
    queries = low(low_back(matmul(inputs, q_weight) + q_bias))
    key_rows = low(low_back(matmul(inputs, k_weight)))
    value_rows = low(low_back(matmul(inputs, v_weight) + v_bias))
    head_q = queries.reshape(LEN, H, HD)
    head_k = key_rows.reshape(LEN, H, HD)
    head_v = value_rows.reshape(LEN, H, HD)
    scores = jnp.einsum('qhd,khd->hqk', head_q, head_k, precision=lax.Precision.HIGHEST) * 0.125
    scores = low_back(scores)
    visible = jnp.arange(LEN).astype(jnp.int32) < length
    scores = jnp.where(visible[None, None, :], scores, -1e+30)
    shifted = scores - lax.optimization_barrier(jnp.max(scores, axis=-1, keepdims=True))
    raised = jnp.exp(shifted)
    shares = raised / lax.optimization_barrier(jnp.sum(raised, axis=-1, keepdims=True))
    context = jnp.einsum('hqk,khd->qhd', low(shares), head_v, precision=lax.Precision.HIGHEST)
    context = low(low_back(context.reshape(LEN, D)))
    resid_a = inputs + low_back(matmul(context, o_weight) + o_bias)
    middle = layer_norm(resid_a, attn_gain, attn_shift)
    pre_act = low_back(matmul(low(middle), in_weight) + in_bias)
    active = low(jax.nn.gelu(pre_act, approximate=False))
    resid_f = middle + low_back(matmul(active, out_weight) + out_bias)
    return layer_norm(resid_f, ffn_gain, ffn_shift)

def reference(tokens, lengths, order, q_weight, k_weight, v_weight, o_weight, q_bias, v_bias, o_bias, attn_gain, attn_shift, in_weight, in_bias, out_weight, out_bias, ffn_gain, ffn_shift, cotangent):
    params = tuple((value.astype(jnp.float32) for value in (q_weight, k_weight, v_weight, o_weight, q_bias, v_bias, o_bias, attn_gain, attn_shift, in_weight, in_bias, out_weight, out_bias, ffn_gain, ffn_shift)))
    slots = order.astype(jnp.int32)
    dealt = jnp.take(tokens, slots, axis=0)
    live = jnp.take(lengths, slots, axis=0)

    def per_sequence(running, members):
        inputs, cotan_rows, length = members

        def apply(param_list, input_rows):
            return forward(param_list, input_rows, length)
        result, pullback = jax.vjp(apply, params, inputs.astype(jnp.float32))
        param_grads, input_grads = pullback(cotan_rows.astype(jnp.float32))
        running = jax.tree.map(lambda first, second: first + second, running, param_grads)
        return (running, (result.astype(jnp.bfloat16), input_grads))
    start = tuple((jnp.zeros(value.shape, jnp.float32) for value in params))
    totals, (output, input_grad) = lax.scan(per_sequence, start, (dealt, cotangent, live))
    return (output, input_grad) + tuple(totals)
```

```python
import functools
import jax, jax.numpy as jnp
from jax import lax
from jax.experimental import pallas as pl
from jax.experimental.pallas import tpu as pltpu
bf=jnp.bfloat16; f32=jnp.float32
HD=64
NEG=-1e30

def _assemble(own_ref, sib_ref, full_ref, c, x, piece):
    rows=own_ref.shape[0]
    for b in range(rows//piece):
        y=x if b==0 else 1-x
        full_ref[pl.ds((2*y+c)*piece,piece),:]=own_ref[b*piece:(b+1)*piece,:]
        full_ref[pl.ds((2*y+1-c)*piece,piece),:]=sib_ref[b*piece:(b+1)*piece,:]

def _masked_rows(t):
    row=lax.broadcasted_iota(jnp.int32,t.shape,0)
    z=jnp.zeros_like(t)
    return jnp.where(row<HD,t,z), jnp.where(row<HD,z,t)
def _masked_lanes(t):
    col=lax.broadcasted_iota(jnp.int32,t.shape,1)
    z=jnp.zeros_like(t)
    return jnp.where(col<HD,t,z), jnp.where(col<HD,z,t)

def dot(a,b): return jnp.dot(a,b,preferred_element_type=f32)

def fwd_kernel(piece, KB, QB, live_ref, q_ref, ko_ref, vo_ref, ks_ref, vs_ref, c_ref, lse_ref,
               kfull, vfull, vT0, vT1, qT0, qT1, acc):
    live=live_ref[0]; c=live_ref[1]; x=live_ref[2]
    _assemble(ko_ref,ks_ref,kfull,c,x,piece)
    _assemble(vo_ref,vs_ref,vfull,c,x,piece)
    L=kfull.shape[0]; nq=q_ref.shape[0]
    for i in range(0,L,512):
        t=jnp.transpose(vfull[i:i+512,:])
        a,b=_masked_rows(t); vT0[:,i:i+512]=a; vT1[:,i:i+512]=b
    for i in range(0,nq,512):
        t=jnp.transpose(q_ref[i:i+512,:]*jnp.asarray(0.125,bf))
        a,b=_masked_rows(t); qT0[:,i:i+512]=a; qT1[:,i:i+512]=b
    nb=(live+KB-1)//KB
    rowsel=lax.broadcasted_iota(jnp.int32,(2*HD,QB),0)<HD
    for qi in range(nq//QB):
        qs=slice(qi*QB,(qi+1)*QB)
        acc[...]=jnp.zeros_like(acc)
        def block(j,carry,masked):
            m0,l0,m1,l1=carry
            ks=pl.multiple_of(j*KB,KB)
            kb=kfull[pl.ds(ks,KB),:]
            s0=dot(kb,qT0[:,qs]); s1=dot(kb,qT1[:,qs])
            if masked:
                keep=lax.broadcasted_iota(jnp.int32,(KB,QB),0)+ks<live
                s0=jnp.where(keep,s0,NEG); s1=jnp.where(keep,s1,NEG)
            n0=jnp.maximum(m0,jnp.max(s0,axis=0,keepdims=True)); n1=jnp.maximum(m1,jnp.max(s1,axis=0,keepdims=True))
            p0=jnp.exp(s0-n0); p1=jnp.exp(s1-n1)
            a0=jnp.exp(m0-n0); a1=jnp.exp(m1-n1)
            l0=l0*a0+jnp.sum(p0,axis=0,keepdims=True); l1=l1*a1+jnp.sum(p1,axis=0,keepdims=True)
            pv=dot(vT0[:,pl.ds(ks,KB)],p0.astype(bf))+dot(vT1[:,pl.ds(ks,KB)],p1.astype(bf))
            acc[...]=acc[...]*jnp.where(rowsel,a0,a1)+pv
            return n0,l0,n1,l1
        init=(jnp.full((1,QB),NEG,f32),jnp.zeros((1,QB),f32))*2
        carry=lax.fori_loop(0,nb-1,lambda j,cr:block(j,cr,False),init)
        m0,l0,m1,l1=block(nb-1,carry,True)
        o=acc[...]*jnp.where(rowsel,1.0/l0,1.0/l1)
        c_ref[qs,:]=jnp.transpose(o).astype(bf)
        lse_ref[0,0:1,qs]=m0+jnp.log(l0); lse_ref[0,1:2,qs]=m1+jnp.log(l1)

def attn_fwd(q, kvo, kvs, sc, piece, KB=256, QB=1024):
    nq,w=q.shape; pairs=w//128; L=2*kvo.shape[0]
    qspec=lambda off: pl.BlockSpec((nq,128),lambda p,s:(0,p+off))
    kspec=lambda off: pl.BlockSpec((L//2,128),lambda p,s:(0,p+off))
    return pl.pallas_call(functools.partial(fwd_kernel,piece,KB,QB),
        grid_spec=pltpu.PrefetchScalarGridSpec(num_scalar_prefetch=1,grid=(pairs,),
            in_specs=[qspec(0),kspec(0),kspec(pairs),kspec(0),kspec(pairs)],
            out_specs=[qspec(0),pl.BlockSpec((1,2,nq),lambda p,s:(p,0,0))],
            scratch_shapes=[pltpu.VMEM((L,128),bf)]*2+[pltpu.VMEM((128,L),bf)]*2+[pltpu.VMEM((128,nq),bf)]*2+[pltpu.VMEM((128,QB),f32)]),
        out_shape=(jax.ShapeDtypeStruct((nq,w),bf),jax.ShapeDtypeStruct((pairs,2,nq),f32)),
        name="attn_fwd",
        cost_estimate=pl.CostEstimate(flops=int(4*nq*L*w*0.6*3),bytes_accessed=6*nq*w*2*2,transcendentals=int(nq*L*w/64*0.6)),
        compiler_params=pltpu.CompilerParams(vmem_limit_bytes=40*2**20,dimension_semantics=("arbitrary",)))(sc,q,kvo,kvo,kvs,kvs)

def bwd_kernel(piece, KB, QB, live_ref, q_ref, ko_ref, vo_ref, ks_ref, vs_ref, c_ref, dc_ref, lse_ref, dq_ref, dko_ref, dvo_ref, dks_ref, dvs_ref,
               kfull, vfull, kT0, kT1, qT0, qT1, dT0, dT1, qm0,qm1,dm0,dm1, delta, dkf, dvf, dqT):
    live=live_ref[0]; c=live_ref[1]; x=live_ref[2]
    _assemble(ko_ref,ks_ref,kfull,c,x,piece)
    _assemble(vo_ref,vs_ref,vfull,c,x,piece)
    L=kfull.shape[0]; nq=q_ref.shape[0]
    for i in range(0,L,512):
        t=jnp.transpose(kfull[i:i+512,:])
        a,b=_masked_rows(t); kT0[:,i:i+512]=a; kT1[:,i:i+512]=b
    for i in range(0,nq,512):
        s=slice(i,i+512)
        qf=q_ref[s,:]*jnp.asarray(0.125,bf)
        a,b=_masked_rows(jnp.transpose(qf)); qT0[:,s]=a; qT1[:,s]=b
        a,b=_masked_lanes(qf); qm0[s,:]=a; qm1[s,:]=b
        d=dc_ref[s,:]; df=d.astype(f32)
        dt=jnp.transpose(d)
        a,b=_masked_rows(dt); dT0[:,s]=a; dT1[:,s]=b
        a,b=_masked_lanes(d); dm0[s,:]=a; dm1[s,:]=b
        prod=jnp.transpose(df*c_ref[s,:].astype(f32))
        delta[0:1,s]=jnp.sum(prod[:HD],axis=0,keepdims=True); delta[1:2,s]=jnp.sum(prod[HD:],axis=0,keepdims=True)
    dqT[...]=jnp.zeros_like(dqT)
    nb=(live+KB-1)//KB
    def zero(j,_):
        ks=pl.multiple_of(j*KB,KB)
        dkf[pl.ds(ks,KB),:]=jnp.zeros((KB,128),bf); dvf[pl.ds(ks,KB),:]=jnp.zeros((KB,128),bf)
        return 0
    lax.fori_loop(nb,L//KB,zero,0)
    def block(j,masked):
        ks=pl.multiple_of(j*KB,KB)
        kb=kfull[pl.ds(ks,KB),:]; vb=vfull[pl.ds(ks,KB),:]
        k0=kT0[:,pl.ds(ks,KB)]; k1=kT1[:,pl.ds(ks,KB)]
        dk=None; dv=None
        for qi in range(nq//QB):
            qs=slice(qi*QB,(qi+1)*QB)
            dq=None
            for qT,dT,qm,dm,kT,h in ((qT0,dT0,qm0,dm0,k0,0),(qT1,dT1,qm1,dm1,k1,1)):
                s=dot(kb,qT[:,qs])
                p=jnp.exp(s-lse_ref[0,h:h+1,qs])
                if masked:
                    keep=lax.broadcasted_iota(jnp.int32,(KB,QB),0)+ks<live
                    p=jnp.where(keep,p,0.0)
                dp=dot(vb,dT[:,qs])
                ds=(p*(dp-delta[h:h+1,qs])).astype(bf)
                v_=dot(p.astype(bf),dm[qs,:]); k_=dot(ds,qm[qs,:]); q_=dot(kT,ds)
                dv=v_ if dv is None else dv+v_
                dk=k_ if dk is None else dk+k_
                dq=q_ if dq is None else dq+q_
            dqT[:,qs]+=dq
        dkf[pl.ds(ks,KB),:]=dk.astype(bf); dvf[pl.ds(ks,KB),:]=dv.astype(bf)
        return 0
    lax.fori_loop(0,nb-1,lambda j,_:block(j,False),0)
    block(nb-1,True)
    for i in range(0,nq,512):
        dq_ref[i:i+512,:]=(jnp.transpose(dqT[:,i:i+512])*0.125).astype(bf)
    for b in range(nq//piece):
        r=slice(b*piece,(b+1)*piece)
        y=x if b==0 else 1-x
        so=pl.ds((2*y+c)*piece,piece); ss=pl.ds((2*y+1-c)*piece,piece)
        dko_ref[r,:]=dkf[so,:]; dks_ref[r,:]=dkf[ss,:]
        dvo_ref[r,:]=dvf[so,:]; dvs_ref[r,:]=dvf[ss,:]

def attn_bwd(q, kvo, kvs, ctx, dctx, lse, sc, piece, KB=256, QB=512):
    nq,w=q.shape; pairs=w//128; L=2*kvo.shape[0]
    qspec=lambda off: pl.BlockSpec((nq,128),lambda p,s:(0,p+off))
    o=jax.ShapeDtypeStruct((nq,w),bf)
    V=pltpu.VMEM
    return pl.pallas_call(functools.partial(bwd_kernel,piece,KB,QB),
        grid_spec=pltpu.PrefetchScalarGridSpec(num_scalar_prefetch=1,grid=(pairs,),
            in_specs=[qspec(0),qspec(0),qspec(pairs),qspec(0),qspec(pairs),qspec(0),qspec(0),pl.BlockSpec((1,2,nq),lambda p,s:(p,0,0))],
            out_specs=[qspec(0)]*5,
            scratch_shapes=[V((L,128),bf)]*2+[V((128,L),bf)]*2+[V((128,nq),bf)]*4+[V((nq,128),bf)]*4+[V((2,nq),f32),V((L,128),bf),V((L,128),bf),V((128,nq),f32)]),
        out_shape=(o,)*5,
        name="attn_bwd",
        cost_estimate=pl.CostEstimate(flops=int(10*nq*L*w*0.6*3),bytes_accessed=12*nq*w*2*2,transcendentals=int(nq*L*w/64*0.6)),
        compiler_params=pltpu.CompilerParams(vmem_limit_bytes=48*2**20,dimension_semantics=("arbitrary",)))(sc,q,kvo,kvo,kvs,kvs,ctx,dctx,lse)

from jax.sharding import PartitionSpec as P
ALL=("dp","mp")
epsilon=1e-5
root_half=0.7071067811865476
inverse_root_two_pi=0.3989422804014327

def norm_forward(values, gain, shift):
    center = jnp.mean(values, axis=-1, keepdims=True)
    offset = values - center
    inverse = lax.rsqrt(jnp.mean(offset * offset, axis=-1, keepdims=True) + epsilon)
    normed = offset * inverse
    return (normed * gain + shift, normed, inverse)

def norm_backward(gradient, normed, inverse, gain):
    scaled = gradient * gain
    centered = (scaled - jnp.mean(scaled, axis=-1, keepdims=True)
        - normed * jnp.mean(scaled * normed, axis=-1, keepdims=True))
    return (inverse * centered, jnp.sum(gradient * normed, axis=0), jnp.sum(gradient, axis=0))

def dotT(a,b): return lax.dot_general(a,b,(((1,),(1,)),((),())),preferred_element_type=f32)
def Tdot(a,b): return lax.dot_general(a,b,(((0,),(0,)),((),())),preferred_element_type=f32)

XP=[(0,2),(2,0),(1,3),(3,1)]
CP=[(0,1),(1,0),(2,3),(3,2)]

def on_device(tokens, lengths, order, q_weight, k_weight, v_weight, o_weight, q_bias, v_bias, o_bias,
    attn_gain, attn_shift, in_weight, in_bias, out_weight, out_bias, ffn_gain, ffn_shift, cotangent):
    micro, rows, D = tokens.shape
    FF = in_weight.shape[1]
    G = lax.axis_size("dp")
    n = G*lax.axis_size("mp")
    g = lax.axis_index("dp"); m = lax.axis_index("mp")
    x = m//2; c = m%2
    sh = q_weight.shape[0]
    hw = D//2
    col = lambda v: v.reshape(sh,1)
    small = jnp.concatenate([col(v) for v in (q_bias,v_bias,o_bias,attn_gain,attn_shift,out_bias,ffn_gain,ffn_shift)]
        + [jnp.transpose(in_bias.reshape(FF//D,sh)), jnp.zeros((sh,128-8-FF//D),bf)],axis=1)
    qkv_l = jnp.concatenate([q_weight,k_weight,v_weight,small],axis=1)
    qkv = lax.all_gather(qkv_l,ALL,axis=0,tiled=True)
    oin = lax.all_gather(jnp.concatenate([o_weight,in_weight],axis=1),ALL,axis=0,tiled=True)
    w_out = lax.all_gather(out_weight,ALL,axis=0,tiled=True)
    w_o, w_in = oin[:,:D], oin[:,D:]
    smalls = jnp.transpose(qkv[:,3*D:])
    qb,vb,ob,ag,ash,outb,fg,fs = [smalls[i].astype(f32) for i in range(8)]
    inb = smalls[8:8+FF//D].reshape(FF//D,n,sh).transpose(1,0,2).reshape(FF).astype(f32)
    cut = lambda i: lax.dynamic_slice(qkv,(0,i*D+x*hw),(D,hw))
    wq,wk,wv = cut(0),cut(1),cut(2)
    qbx = lax.dynamic_slice(qb,(x*hw,),(hw,)); vbx = lax.dynamic_slice(vb,(x*hw,),(hw,))
    R = rows//G
    mixed = lax.all_to_all(tokens.reshape(micro,G,R,D),"dp",split_axis=1,concat_axis=0,tiled=True).reshape(micro*G,R,D)
    picked = jnp.take(mixed,order,axis=0).reshape(G,micro,R,D)
    live_all = jnp.take(lengths,order,axis=0)
    outs=[];igs=[]
    st=[]
    for s in range(micro):
        own = lax.all_to_all(picked[:,s],"dp",split_axis=0,concat_axis=0,tiled=True).reshape(rows,D)
        oth = lax.ppermute(own,"mp",XP)
        X = jnp.concatenate([own,oth],axis=0)
        live = live_all[g*micro+s]
        sc = jnp.stack([live,c,x]).astype(jnp.int32)
        q = (jnp.dot(X,wq,preferred_element_type=f32)+qbx).astype(bf)
        k = jnp.dot(X,wk,preferred_element_type=f32).astype(bf)
        v = (jnp.dot(X,wv,preferred_element_type=f32)+vbx).astype(bf)
        kvo = jnp.concatenate([k,v],axis=1)
        kvs = lax.ppermute(kvo,"mp",CP)
        ctx,lse = attn_fwd(q,kvo,kvs,sc,rows)
        c_oth = lax.ppermute(ctx[rows:],"mp",XP)
        st.append([own,X,sc,q,kvo,kvs,ctx,lse,c_oth])
    dW=None
    st2=[]
    for s in range(micro):
        own,X,sc,q,kvo,kvs,ctx,lse,c_oth = st[s]
        mine = ctx[:rows]
        cfull = jnp.where(x==0,jnp.concatenate([mine,c_oth],axis=1),jnp.concatenate([c_oth,mine],axis=1))
        A = own.astype(f32)+jnp.dot(cfull,w_o,preferred_element_type=f32)+ob
        U,n1,r1 = norm_forward(A,ag,ash)
        ul = U.astype(bf)
        F = jnp.dot(ul,w_in,preferred_element_type=f32)+inb
        Z = jax.nn.gelu(F,approximate=False).astype(bf)
        B = U+jnp.dot(Z,w_out,preferred_element_type=f32)+outb
        out,n2,r2 = norm_forward(B,fg,fs)
        outs.append(out.astype(bf))
        G_ = cotangent[s].astype(f32)
        dB,dfg,dfs = norm_backward(G_,n2,r2,fg)
        dO = dB.astype(bf)
        doutb = jnp.sum(dO.astype(f32),axis=0)
        dwout = Tdot(Z,dO)
        dZ = dotT(dO,w_out)
        slope = 0.5*(1.0+lax.erf(F*root_half))+F*jnp.exp(-0.5*F*F)*inverse_root_two_pi
        dF = (dZ*slope).astype(bf)
        dinb = jnp.sum(dF.astype(f32),axis=0)
        dwin = Tdot(ul,dF)
        dU = dB+dotT(dF,w_in)
        dA,dag,dash = norm_backward(dU,n1,r1,ag)
        dM = dA.astype(bf)
        dob = jnp.sum(dM.astype(f32),axis=0)
        dwo = Tdot(cfull,dM)
        dC = dotT(dM,w_o).astype(bf)
        dc_l,dc_r = dC[:,:hw],dC[:,hw:]
        keep = jnp.where(x==0,dc_l,dc_r); send = jnp.where(x==0,dc_r,dc_l)
        got = lax.ppermute(send,"mp",XP)
        st2.append((dA,jnp.concatenate([keep,got],axis=0)))
        now = [dwo,dwin,dwout,dob,dag,dash,doutb,dfg,dfs,dinb]
        dW = now if dW is None else [a+b for a,b in zip(dW,now)]
    dQKV=None
    for s in range(micro):
        own,X,sc,q,kvo,kvs,ctx,lse,c_oth = st[s]
        dA,dctx = st2[s]
        dq,dko,dvo,dks,dvs = attn_bwd(q,kvo,kvs,ctx,dctx,lse,sc,rows)
        r_ = lax.ppermute(jnp.concatenate([dks,dvs],axis=1),"mp",CP)
        dk = (dko.astype(f32)+r_[:,:hw].astype(f32)).astype(bf)
        dv = (dvo.astype(f32)+r_[:,hw:].astype(f32)).astype(bf)
        dXp = dotT(dq,wq)+dotT(dk,wk)+dotT(dv,wv)
        rx = lax.ppermute(dXp[rows:].astype(bf),"mp",XP)
        igs.append(dA+dXp[:rows]+rx.astype(f32))
        now = [Tdot(X,dq),Tdot(X,dk),Tdot(X,dv),jnp.sum(dq.astype(f32),axis=0),jnp.sum(dv.astype(f32),axis=0)]
        dQKV = now if dQKV is None else [a+b for a,b in zip(dQKV,now)]
    wide = lambda t: lax.dynamic_update_slice(jnp.zeros(t.shape[:-1]+(D,),bf),t.astype(bf),(0,)*(t.ndim-1)+(x*hw,))
    dwq,dwk,dwv,dqb,dvb = [wide(t) for t in dQKV]
    dwo,dwin,dwout,dob,dag,dash,doutb,dfg,dfs,dinb = [t.astype(bf) for t in dW]
    dsm = jnp.concatenate([jnp.stack([dqb,dvb,dob,dag,dash,doutb,dfg,dfs]),
        dinb.reshape(n,FF//D,sh).transpose(1,0,2).reshape(FF//D,D), jnp.zeros((128-8-FF//D,D),bf)],axis=0)
    dwo2 = dwout.reshape(n,FF//D,sh,D).transpose(0,2,1,3).reshape(D,FF)
    big = jnp.concatenate([dwq,dwk,dwv,dwo,dwin,dwo2,jnp.transpose(dsm)],axis=1)
    red = lax.psum_scatter(big,ALL,scatter_dimension=0,tiled=True).astype(f32)
    pick = lambda i: red[:,i*D:(i+1)*D]
    gin = red[:,4*D:4*D+FF]
    gout = red[:,4*D+FF:4*D+2*FF].reshape(sh,FF//D,D).transpose(1,0,2).reshape(sh*(FF//D),D)
    sm = jnp.transpose(red[:,4*D+2*FF:])
    ginb = sm[8:8+FF//D].reshape(-1)
    return (jnp.stack(outs),jnp.stack(igs),pick(0),pick(1),pick(2),pick(3),sm[0],sm[1],sm[2],sm[3],sm[4],gin,ginb,gout,sm[5],sm[6],sm[7])

def solution(mesh):
    r2=P(ALL,None); r1=P(ALL); t=P("dp","mp",None)
    return jax.shard_map(on_device,mesh=mesh,
        in_specs=(t,P(),P(),r2,r2,r2,r2,r1,r1,r1,r1,r1,r2,r1,r2,r1,r1,r1,t),
        out_specs=(t,t,r2,r2,r2,r2,r1,r1,r1,r1,r1,r2,r1,r2,r1,r1,r1),check_vma=False)
```

```python
import functools
import jax, jax.numpy as jnp
from jax import lax
from jax.experimental import pallas as pl
from jax.experimental.pallas import tpu as pltpu
bf=jnp.bfloat16; f32=jnp.float32
HD=64
NEG=-1e30

def _assemble(own_ref, sib_ref, full_ref, c, x, piece):
    rows=own_ref.shape[0]
    for b in range(rows//piece):
        y=x if b==0 else 1-x
        full_ref[pl.ds((2*y+c)*piece,piece),:]=own_ref[b*piece:(b+1)*piece,:]
        full_ref[pl.ds((2*y+1-c)*piece,piece),:]=sib_ref[b*piece:(b+1)*piece,:]

def _masked_rows(t):
    row=lax.broadcasted_iota(jnp.int32,t.shape,0)
    z=jnp.zeros_like(t)
    return jnp.where(row<HD,t,z), jnp.where(row<HD,z,t)
def _masked_lanes(t):
    col=lax.broadcasted_iota(jnp.int32,t.shape,1)
    z=jnp.zeros_like(t)
    return jnp.where(col<HD,t,z), jnp.where(col<HD,z,t)


def fwd_kernel(piece, KB, QB, live_ref, q_ref, ko_ref, vo_ref, ks_ref, vs_ref, c_ref, lse_ref,
               kfull, vfull, vT0, vT1, qT0, qT1, acc):
    live=live_ref[0]; c=live_ref[1]; x=live_ref[2]
    _assemble(ko_ref,ks_ref,kfull,c,x,piece)
    _assemble(vo_ref,vs_ref,vfull,c,x,piece)
    L=kfull.shape[0]; nq=q_ref.shape[0]
    for i in range(0,L,512):
        t=jnp.transpose(vfull[i:i+512,:])
        a,b=_masked_rows(t); vT0[:,i:i+512]=a; vT1[:,i:i+512]=b
    for i in range(0,nq,512):
        t=jnp.transpose(q_ref[i:i+512,:]*jnp.asarray(0.125,bf))
        a,b=_masked_rows(t); qT0[:,i:i+512]=a; qT1[:,i:i+512]=b
    nb=(live+KB-1)//KB
    rowsel=lax.broadcasted_iota(jnp.int32,(2*HD,QB),0)<HD
    for qi in range(nq//QB):
        qs=slice(qi*QB,(qi+1)*QB)
        acc[...]=jnp.zeros_like(acc)
        def block(j,carry,masked):
            m0,l0,m1,l1=carry
            ks=pl.multiple_of(j*KB,KB)
            kb=kfull[pl.ds(ks,KB),:]
            s0=dot(kb,qT0[:,qs]); s1=dot(kb,qT1[:,qs])
            if masked:
                keep=lax.broadcasted_iota(jnp.int32,(KB,QB),0)+ks<live
                s0=jnp.where(keep,s0,NEG); s1=jnp.where(keep,s1,NEG)
            n0=jnp.maximum(m0,jnp.max(s0,axis=0,keepdims=True)); n1=jnp.maximum(m1,jnp.max(s1,axis=0,keepdims=True))
            p0=jnp.exp(s0-n0); p1=jnp.exp(s1-n1)
            a0=jnp.exp(m0-n0); a1=jnp.exp(m1-n1)
            l0=l0*a0+jnp.sum(p0,axis=0,keepdims=True); l1=l1*a1+jnp.sum(p1,axis=0,keepdims=True)
            pv=dot(vT0[:,pl.ds(ks,KB)],p0.astype(bf))+dot(vT1[:,pl.ds(ks,KB)],p1.astype(bf))
            acc[...]=acc[...]*jnp.where(rowsel,a0,a1)+pv
            return n0,l0,n1,l1
        init=(jnp.full((1,QB),NEG,f32),jnp.zeros((1,QB),f32))*2
        carry=lax.fori_loop(0,nb-1,lambda j,cr:block(j,cr,False),init)
        m0,l0,m1,l1=block(nb-1,carry,True)
        o=acc[...]*jnp.where(rowsel,1.0/l0,1.0/l1)
        c_ref[qs,:]=jnp.transpose(o).astype(bf)
        lse_ref[0,0:1,qs]=m0+jnp.log(l0); lse_ref[0,1:2,qs]=m1+jnp.log(l1)

def attn_fwd(q, kvo, kvs, sc, piece, KB=256, QB=1024):
    nq,w=q.shape; pairs=w//128; L=2*kvo.shape[0]
    qspec=lambda off: pl.BlockSpec((nq,128),lambda p,s:(0,p+off))
    kspec=lambda off: pl.BlockSpec((L//2,128),lambda p,s:(0,p+off))
    return pl.pallas_call(functools.partial(fwd_kernel,piece,KB,QB),
        grid_spec=pltpu.PrefetchScalarGridSpec(num_scalar_prefetch=1,grid=(pairs,),
            in_specs=[qspec(0),kspec(0),kspec(pairs),kspec(0),kspec(pairs)],
            out_specs=[qspec(0),pl.BlockSpec((1,2,nq),lambda p,s:(p,0,0))],
            scratch_shapes=[pltpu.VMEM((L,128),bf)]*2+[pltpu.VMEM((128,L),bf)]*2+[pltpu.VMEM((128,nq),bf)]*2+[pltpu.VMEM((128,QB),f32)]),
        out_shape=(jax.ShapeDtypeStruct((nq,w),bf),jax.ShapeDtypeStruct((pairs,2,nq),f32)),
        name="attn_fwd",
        cost_estimate=pl.CostEstimate(flops=int(4*nq*L*w*0.6*3),bytes_accessed=6*nq*w*2*2,transcendentals=int(nq*L*w/64*0.6)),
        compiler_params=pltpu.CompilerParams(vmem_limit_bytes=40*2**20,dimension_semantics=("arbitrary",)))(sc,q,kvo,kvo,kvs,kvs)

def bwd_kernel(piece, KB, QB, live_ref, q_ref, ko_ref, vo_ref, ks_ref, vs_ref, c_ref, dc_ref, lse_ref, dq_ref, dko_ref, dvo_ref, dks_ref, dvs_ref,
               kfull, vfull, kT0, kT1, qT0, qT1, dT0, dT1, qm0,qm1,dm0,dm1, delta, dkf, dvf, dqT):
    live=live_ref[0]; c=live_ref[1]; x=live_ref[2]
    _assemble(ko_ref,ks_ref,kfull,c,x,piece)
    _assemble(vo_ref,vs_ref,vfull,c,x,piece)
    L=kfull.shape[0]; nq=q_ref.shape[0]
    for i in range(0,L,512):
        t=jnp.transpose(kfull[i:i+512,:])
        a,b=_masked_rows(t); kT0[:,i:i+512]=a; kT1[:,i:i+512]=b
    for i in range(0,nq,512):
        s=slice(i,i+512)
        qf=q_ref[s,:]*jnp.asarray(0.125,bf)
        a,b=_masked_rows(jnp.transpose(qf)); qT0[:,s]=a; qT1[:,s]=b
        a,b=_masked_lanes(qf); qm0[s,:]=a; qm1[s,:]=b
        d=dc_ref[s,:]; df=d.astype(f32)
        dt=jnp.transpose(d)
        a,b=_masked_rows(dt); dT0[:,s]=a; dT1[:,s]=b
        a,b=_masked_lanes(d); dm0[s,:]=a; dm1[s,:]=b
        prod=jnp.transpose(df*c_ref[s,:].astype(f32))
        delta[0:1,s]=jnp.sum(prod[:HD],axis=0,keepdims=True); delta[1:2,s]=jnp.sum(prod[HD:],axis=0,keepdims=True)
    dqT[...]=jnp.zeros_like(dqT)
    nb=(live+KB-1)//KB
    def zero(j,_):
        ks=pl.multiple_of(j*KB,KB)
        dkf[pl.ds(ks,KB),:]=jnp.zeros((KB,128),bf); dvf[pl.ds(ks,KB),:]=jnp.zeros((KB,128),bf)
        return 0
    lax.fori_loop(nb,L//KB,zero,0)
    def block(j,masked):
        ks=pl.multiple_of(j*KB,KB)
        kb=kfull[pl.ds(ks,KB),:]; vb=vfull[pl.ds(ks,KB),:]
        k0=kT0[:,pl.ds(ks,KB)]; k1=kT1[:,pl.ds(ks,KB)]
        dk=None; dv=None
        for qi in range(nq//QB):
            qs=slice(qi*QB,(qi+1)*QB)
            dq=None
            for qT,dT,qm,dm,kT,h in ((qT0,dT0,qm0,dm0,k0,0),(qT1,dT1,qm1,dm1,k1,1)):
                s=dot(kb,qT[:,qs])
                p=jnp.exp(s-lse_ref[0,h:h+1,qs])
                if masked:
                    keep=lax.broadcasted_iota(jnp.int32,(KB,QB),0)+ks<live
                    p=jnp.where(keep,p,0.0)
                dp=dot(vb,dT[:,qs])
                ds=(p*(dp-delta[h:h+1,qs])).astype(bf)
                v_=dot(p.astype(bf),dm[qs,:]); k_=dot(ds,qm[qs,:]); q_=dot(kT,ds)
                dv=v_ if dv is None else dv+v_
                dk=k_ if dk is None else dk+k_
                dq=q_ if dq is None else dq+q_
            dqT[:,qs]+=dq
        dkf[pl.ds(ks,KB),:]=dk.astype(bf); dvf[pl.ds(ks,KB),:]=dv.astype(bf)
        return 0
    lax.fori_loop(0,nb-1,lambda j,_:block(j,False),0)
    block(nb-1,True)
    for i in range(0,nq,512):
        dq_ref[i:i+512,:]=(jnp.transpose(dqT[:,i:i+512])*0.125).astype(bf)
    for b in range(nq//piece):
        r=slice(b*piece,(b+1)*piece)
        y=x if b==0 else 1-x
        so=pl.ds((2*y+c)*piece,piece); ss=pl.ds((2*y+1-c)*piece,piece)
        dko_ref[r,:]=dkf[so,:]; dks_ref[r,:]=dkf[ss,:]
        dvo_ref[r,:]=dvf[so,:]; dvs_ref[r,:]=dvf[ss,:]

def attn_bwd(q, kvo, kvs, ctx, dctx, lse, sc, piece, KB=256, QB=512):
    nq,w=q.shape; pairs=w//128; L=2*kvo.shape[0]
    qspec=lambda off: pl.BlockSpec((nq,128),lambda p,s:(0,p+off))
    o=jax.ShapeDtypeStruct((nq,w),bf)
    V=pltpu.VMEM
    return pl.pallas_call(functools.partial(bwd_kernel,piece,KB,QB),
        grid_spec=pltpu.PrefetchScalarGridSpec(num_scalar_prefetch=1,grid=(pairs,),
            in_specs=[qspec(0),qspec(0),qspec(pairs),qspec(0),qspec(pairs),qspec(0),qspec(0),pl.BlockSpec((1,2,nq),lambda p,s:(p,0,0))],
            out_specs=[qspec(0)]*5,
            scratch_shapes=[V((L,128),bf)]*2+[V((128,L),bf)]*2+[V((128,nq),bf)]*4+[V((nq,128),bf)]*4+[V((2,nq),f32),V((L,128),bf),V((L,128),bf),V((128,nq),f32)]),
        out_shape=(o,)*5,
        name="attn_bwd",
        cost_estimate=pl.CostEstimate(flops=int(10*nq*L*w*0.6*3),bytes_accessed=12*nq*w*2*2,transcendentals=int(nq*L*w/64*0.6)),
        compiler_params=pltpu.CompilerParams(vmem_limit_bytes=48*2**20,dimension_semantics=("arbitrary",)))(sc,q,kvo,kvo,kvs,kvs,ctx,dctx,lse)

NTd=(((1,),(1,)),((),())); TNd=(((0,),(0,)),((),()))
def dot(a,b): return jnp.dot(a,b,preferred_element_type=f32)
def dotT(a,b): return lax.dot_general(a,b,NTd,preferred_element_type=f32)
def Tdot(a,b): return lax.dot_general(a,b,TNd,preferred_element_type=f32)
epsilon=1e-5
root_half=0.7071067811865476
inverse_root_two_pi=0.3989422804014327

def ffn_kernel(T, RC, sc_ref, tok_ref, cm_ref, co_ref, cot_ref, wo_ref, win_ref, wout_ref, vec_ref, inb_ref,
        out_ref, da_ref, dck_ref, dcs_ref, gwo_hbm, gwin_hbm, gwout_hbm, gsm_ref, ginb_ref,
        gwo, gwin, gwout, n1_s, r1_s, ul_s, acc, db_s, do_s, z_s, sl_s, fb, sem):
    s=pl.program_id(0); ns=pl.num_programs(0)
    x=sc_ref[0]
    rows,D=tok_ref.shape[1:]; FF=win_ref.shape[1]; hw=cm_ref.shape[2]
    xs=pl.ds(pl.multiple_of(x*hw,hw),hw); ys=pl.ds(pl.multiple_of((1-x)*hw,hw),hw)
    ob,ag,ash,outb,fg,fs=[vec_ref[i:i+1,:] for i in range(6)]
    @pl.when(s==0)
    def _():
        gsm_ref[...]=jnp.zeros_like(gsm_ref); ginb_ref[...]=jnp.zeros_like(ginb_ref)
    nr=rows//RC
    def p1(i,_):
        r=pl.ds(pl.multiple_of(i*RC,RC),RC)
        a=tok_ref[0,r,:].astype(f32)+dot(cm_ref[0,r,:],wo_ref[xs,:])+dot(co_ref[0,r,:],wo_ref[ys,:])+ob
        o=a-jnp.mean(a,axis=-1,keepdims=True)
        inv=lax.rsqrt(jnp.mean(o*o,axis=-1,keepdims=True)+epsilon)
        n=o*inv
        n1_s[r,:]=n; r1_s[r,:]=jnp.broadcast_to(inv,(RC,128))
        ul_s[r,:]=(n*ag+ash).astype(bf)
        return 0
    lax.fori_loop(0,nr,p1,0)
    nt=FF//T
    def mm1(t): return dot(ul_s[...],win_ref[:,pl.ds(pl.multiple_of(t*T,T),T)])
    fb[0]=mm1(0)
    def p2(t,_):
        ts=pl.ds(pl.multiple_of(t*T,T),T)
        @pl.when(t+1<nt)
        def _(): pass
        nxt=jnp.minimum(t+1,nt-1)
        fnext=mm1(nxt)
        f=fb[lax.rem(t,2)]+inb_ref[:,ts]
        cdf=0.5*(1.0+lax.erf(f*root_half))
        pdf=jnp.exp(-0.5*f*f)*inverse_root_two_pi
        z=(f*cdf).astype(bf)
        z_s[:,ts]=z; sl_s[:,ts]=(cdf+f*pdf).astype(bf)
        y=dot(z,wout_ref[ts,:])
        fb[lax.rem(t+1,2)]=fnext
        @pl.when(t==0)
        def _(): acc[...]=y
        @pl.when(t>0)
        def _(): acc[...]+=y
        return 0
    lax.fori_loop(0,nt,p2,0)
    def p3(i,_):
        r=pl.ds(pl.multiple_of(i*RC,RC),RC)
        b=acc[r,:]+(n1_s[r,:]*ag+ash)+outb
        o=b-jnp.mean(b,axis=-1,keepdims=True)
        inv=lax.rsqrt(jnp.mean(o*o,axis=-1,keepdims=True)+epsilon)
        n=o*inv
        out_ref[0,r,:]=(n*fg+fs).astype(bf)
        g=cot_ref[0,r,:].astype(f32)
        e=g*fg
        db=inv*(e-jnp.mean(e,axis=-1,keepdims=True)-n*jnp.mean(e*n,axis=-1,keepdims=True))
        db_s[r,:]=db
        do=db.astype(bf); do_s[r,:]=do
        gsm_ref[3:4,:]+=jnp.sum(do.astype(f32),axis=0,keepdims=True)
        gsm_ref[4:5,:]+=jnp.sum(g*n,axis=0,keepdims=True)
        gsm_ref[5:6,:]+=jnp.sum(g,axis=0,keepdims=True)
        return 0
    lax.fori_loop(0,nr,p3,0)
    def put(ref,idx,val):
        @pl.when(s==0)
        def _(): ref[idx]=val.astype(bf)
        @pl.when(s>0)
        def _(): ref[idx]=(ref[idx].astype(f32)+val).astype(bf)
    def p4(t,_):
        ts=pl.ds(pl.multiple_of(t*T,T),T)
        dz=dotT(do_s[...],wout_ref[ts,:])
        df=(dz*sl_s[:,ts].astype(f32)).astype(bf)
        put(gwout,(ts,slice(None)),Tdot(z_s[:,ts],do_s[...]))
        put(gwin,(slice(None),ts),Tdot(ul_s[...],df))
        y=dotT(df,win_ref[:,ts])
        ginb_ref[:,ts]+=jnp.sum(df.astype(f32),axis=0,keepdims=True)
        db_s[...]+=y
        return 0
    lax.fori_loop(0,nt,p4,0)
    @pl.when(s==ns-1)
    def _():
        pltpu.make_async_copy(gwin,gwin_hbm,sem.at[0]).start()
        pltpu.make_async_copy(gwout,gwout_hbm,sem.at[1]).start()
    def p5(i,_):
        r=pl.ds(pl.multiple_of(i*RC,RC),RC)
        du=db_s[r,:]; n=n1_s[r,:]; inv=r1_s[r,0:1]
        e=du*ag
        da=inv*(e-jnp.mean(e,axis=-1,keepdims=True)-n*jnp.mean(e*n,axis=-1,keepdims=True))
        da_ref[0,r,:]=da
        dm=da.astype(bf); do_s[r,:]=dm
        gsm_ref[0:1,:]+=jnp.sum(dm.astype(f32),axis=0,keepdims=True)
        gsm_ref[1:2,:]+=jnp.sum(du*n,axis=0,keepdims=True)
        gsm_ref[2:3,:]+=jnp.sum(du,axis=0,keepdims=True)
        dck_ref[0,r,:]=dotT(dm,wo_ref[xs,:]).astype(bf)
        dcs_ref[0,r,:]=dotT(dm,wo_ref[ys,:]).astype(bf)
        return 0
    lax.fori_loop(0,nr,p5,0)
    put(gwo,(xs,slice(None)),Tdot(cm_ref[0],do_s[...]))
    put(gwo,(ys,slice(None)),Tdot(co_ref[0],do_s[...]))
    @pl.when(s==ns-1)
    def _():
        pltpu.make_async_copy(gwo,gwo_hbm,sem.at[2]).start()
        pltpu.make_async_copy(gwin,gwin_hbm,sem.at[0]).wait()
        pltpu.make_async_copy(gwout,gwout_hbm,sem.at[1]).wait()
        pltpu.make_async_copy(gwo,gwo_hbm,sem.at[2]).wait()

def ffn(xi, tok, cm, co, cot, wo, win, wout, vec, inb, T=512, RC=128):
    S,rows,D=tok.shape; FF=win.shape[1]; hw=cm.shape[2]
    V=pltpu.VMEM
    slot=lambda w: pl.BlockSpec((1,rows,w),lambda s,p:(s,0,0))
    full=lambda a: pl.BlockSpec(a.shape,lambda s,p:(0,)*a.ndim,pipeline_mode=pl.Buffered(1))
    anys=pl.BlockSpec(memory_space=pl.ANY)
    sd=jax.ShapeDtypeStruct
    fl=S*rows*D*(2*D+4*FF)*3
    return pl.pallas_call(functools.partial(ffn_kernel,T,RC),
        grid_spec=pltpu.PrefetchScalarGridSpec(num_scalar_prefetch=1,grid=(S,),
            in_specs=[slot(D),slot(hw),slot(hw),slot(D),full(wo),full(win),full(wout),full(vec),full(inb)],
            out_specs=[slot(D),slot(D),slot(hw),slot(hw),anys,anys,anys,pl.BlockSpec((8,D),lambda s,p:(0,0)),pl.BlockSpec((1,FF),lambda s,p:(0,0))],
            scratch_shapes=[V((D,D),bf),V((D,FF),bf),V((FF,D),bf),V((rows,D),f32),V((rows,128),f32),V((rows,D),bf),V((rows,D),f32),V((rows,D),f32),V((rows,D),bf),
                V((rows,FF),bf),V((rows,FF),bf),V((2,rows,T),f32),pltpu.SemaphoreType.DMA((3,))]),
        out_shape=(sd((S,rows,D),bf),sd((S,rows,D),f32),sd((S,rows,hw),bf),sd((S,rows,hw),bf),sd((D,D),bf),sd((D,FF),bf),sd((FF,D),bf),sd((8,D),f32),sd((1,FF),f32)),
        name="ffn",
        cost_estimate=pl.CostEstimate(flops=int(fl),bytes_accessed=40*2**20,transcendentals=2*S*rows*FF),
        compiler_params=pltpu.CompilerParams(vmem_limit_bytes=62*2**20,dimension_semantics=("arbitrary",)))(xi,tok,cm,co,cot,wo,win,wout,vec,inb)

def qkvb_kernel(last, RC, sc_ref, x_ref, dq_ref, dko_ref, dvo_ref, r_ref, da_ref, w_ref, prev_ref, s_ref, ig_ref, dxo_ref, dw_ref, dqkv, accw):
    rows,D=x_ref.shape; hw=dq_ref.shape[1]; half=rows//2
    x=sc_ref[0]
    for i in range(rows//RC):
        r=slice(i*RC,(i+1)*RC)
        dqkv[r,0:hw]=dq_ref[r,:]
        dqkv[r,hw:2*hw]=(dko_ref[r,:].astype(f32)+r_ref[r,0:hw].astype(f32)).astype(bf)
        dqkv[r,2*hw:3*hw]=(dvo_ref[r,:].astype(f32)+r_ref[r,hw:2*hw].astype(f32)).astype(bf)
    for i in range(rows//RC):
        r=slice(i*RC,(i+1)*RC)
        dx=dotT(dqkv[r,:],w_ref[:,0:3*hw])
        if i*RC<half: ig_ref[r,:]=da_ref[r,:]+dx
        else: dxo_ref[i*RC-half:(i+1)*RC-half,:]=dx.astype(bf)
    W=3*hw
    for j in range(3):
        cs=slice(j*hw,(j+1)*hw)
        v=Tdot(x_ref[...],dqkv[:,cs])+prev_ref[:,cs]
        dw_ref[:,cs]=v.astype(dw_ref.dtype)
    ones=jnp.ones((rows,128),bf)
    col=lax.broadcasted_iota(jnp.int32,(hw,128),1)
    b=jnp.where(col==0,Tdot(dqkv[:,0:hw],ones),0.0)+jnp.where(col==1,Tdot(dqkv[:,2*hw:],ones),0.0)
    xs=pl.ds(pl.multiple_of(x*hw,hw),hw)
    if last:
        accw[...]=prev_ref[:,W:]+jnp.transpose(s_ref[...])
        accw[xs,:]+=b
        dw_ref[:,W:]=accw[...].astype(bf)
    else:
        dw_ref[:,W:]=jnp.zeros_like(accw)
        dw_ref[xs,W:]=b

def qkvb(last, xi, X, dq, dko, dvo, r, da, w, prev, small, RC=256):
    rows,D=X.shape; hw=dq.shape[1]; W=3*hw+128
    sd=jax.ShapeDtypeStruct; V=pltpu.VMEM
    vm=pl.BlockSpec(memory_space=pltpu.VMEM)
    return pl.pallas_call(functools.partial(qkvb_kernel,last,RC),
        grid_spec=pltpu.PrefetchScalarGridSpec(num_scalar_prefetch=1,grid=(),in_specs=[vm]*9,out_specs=[vm]*3,
            scratch_shapes=[V((rows,3*hw),bf),V((D,128),f32)]),
        out_shape=(sd((rows//2,D),f32),sd((rows//2,D),bf),sd((D,W),bf if last else f32)),
        name="qkvb_last" if last else "qkvb",
        cost_estimate=pl.CostEstimate(flops=4*rows*D*3*hw,bytes_accessed=20*2**20,transcendentals=0),
        compiler_params=pltpu.CompilerParams(vmem_limit_bytes=48*2**20))(xi,X,dq,dko,dvo,r,da,w,prev,small)

MESH=pl.DeviceIdType.MESH
def reduce_kernel(Z, gin, gout, go, gq, dxo, o_in, o_out, o_o, o_q, o_k, o_v, o_s, rx,
        a1,a2,a3,a4, c1,c2,c3,c4, p1,p2,p3,p4, u1,u2,u3, f1,f2,f3,f4, xb, xr, lsem, ssem, rsem):
    g=lax.axis_index("dp"); m=lax.axis_index("mp")
    h=g//2; y=lax.rem(g,2); x=m//2; c=lax.rem(m,2)
    core={"dp":g,"mp":2*x+1-c}; xn={"dp":g,"mp":2*(1-x)+c}; yn={"dp":2*h+1-y,"mp":m}
    zz=[lax.rem(h+1+t,Z) for t in range(Z)]
    zn=[{"dp":2*zz[t]+y,"mp":m} for t in range(Z)]
    bar=pltpu.get_barrier_semaphore()
    def greet(dev): pl.semaphore_signal(bar,inc=1,device_id=dev,device_id_type=MESH)
    greet(core); greet(xn); greet(yn)
    for t in range(Z-1): greet(zn[t])
    pl.semaphore_wait(bar,3+Z-1)
    A=[a1,a2,a3,a4]; C=[c1,c2,c3,c4]; Pb=[p1,p2,p3,p4]; U=[u1,u2,u3]; F=[f1,f2,f3,f4]; G=[gin,gout,go,gq]
    def rc(src,dst,a,s,t,dev):
        return pltpu.make_async_remote_copy(src_ref=src,dst_ref=dst,send_sem=ssem.at[a,s,t],recv_sem=rsem.at[a,s,t],device_id=dev,device_id_type=MESH)
    pend=[]
    def go_(d): d.start(); pend.append(d); return d
    xd=rc(dxo,rx,0,4,0,xn)
    order=[3,0,1,2]
    core_d={}; loc={}
    for t in range(Z):
        for a in order:
            d=rc(G[a].at[zz[t],:,:,1-c],C[a].at[t],a,0,t,core); d.start(); core_d[a,t]=d
            l=pltpu.make_async_copy(G[a].at[zz[t],:,:,c],A[a].at[t],lsem.at[a,t]); l.start(); loc[a,t]=l
        if t==0: xd.start()
    def add(ref,idx,other):
        ref[idx]=(ref[idx].astype(f32)+other.astype(f32)).astype(bf)
    s1={};s2={};s3={}
    def stage0(t):
        for a in order:
            loc[a,t].wait(); core_d[a,t].wait_recv()
            A[a][t]=(A[a][t].astype(f32)+C[a][t].astype(f32)).astype(bf)
            if a==0: d=rc(A[a].at[t,:,1-x],Pb[a].at[t],a,1,t,xn)
            else: d=rc(A[a].at[t,1-y],Pb[a].at[t],a,1,t,yn)
            d.start(); s1[a,t]=d
    def stage1(t):
        for a in order:
            s1[a,t].wait_recv()
            if a==0:
                for k in range(2): add(A[a],(t,k,x),Pb[a][t,k])
                d=rc(A[a].at[t,1-y,x],U[a].at[t],a,2,t,yn)
            else:
                for k in range(2): add(A[a],(t,y,k),Pb[a][t,k])
                if a==3:
                    if t<Z-1:
                        d=rc(A[a].at[t,y],F[a].at[t],a,3,t,zn[t])
                    else: d=None
                else: d=rc(A[a].at[t,y,1-x],U[a].at[t],a,2,t,xn)
            if d is not None:
                d.start()
                if a==3: s3[a,t]=d
                else: s2[a,t]=d
    def stage2(t):
        for a in (0,1,2):
            s2[a,t].wait_recv()
            add(A[a],(t,y,x),U[a][t])
            if t<Z-1:
                d=rc(A[a].at[t,y,x],F[a].at[t],a,3,t,zn[t]); d.start(); s3[a,t]=d
    for t in range(Z+2):
        if t<Z: stage0(t)
        if 0<=t-1<Z: stage1(t-1)
        if 0<=t-2<Z: stage2(t-2)
    for t in range(Z-1): s3[3,t].wait_recv()
    hw=(gq.shape[-1]-128)//3
    def fin4(k):
        v=a4[Z-1,y,k].astype(f32)
        for t in range(Z-1): v=v+f4[t,k].astype(f32)
        return v
    xb[...]=fin4(1-x).astype(bf)
    xd4=rc(xb,xr,3,2,0,xn); xd4.start()
    for a,o in ((0,o_in),(1,o_out),(2,o_o)):
        v=A[a][Z-1,y,x].astype(f32)
        for t in range(Z-1):
            s3[a,t].wait_recv(); v=v+F[a][t].astype(f32)
        o[...]=v
    mine=fin4(x)
    xs=pl.ds(pl.multiple_of(x*hw,hw),hw); ys=pl.ds(pl.multiple_of((1-x)*hw,hw),hw)
    xd4.wait_recv()
    for i,o in enumerate((o_q,o_k,o_v)):
        o[:,xs]=mine[:,i*hw:(i+1)*hw]
        o[:,ys]=xr[:,i*hw:(i+1)*hw].astype(f32)
    o_s[...]=mine[:,3*hw:]+xr[:,3*hw:].astype(f32)
    xd.wait()
    xd4.wait_send()
    for dd in (core_d,s1,s2,s3):
        for d in dd.values(): d.wait_send()

def reduce_grads(G, gin, gout, go, gq, dxo):
    Z=G//2
    n=4*G
    sd=jax.ShapeDtypeStruct; V=pltpu.VMEM
    arrs=[]
    for a in (gin,gout,go,gq):
        arrs.append(a.reshape(Z,2,2,2,a.shape[0]//n,a.shape[1]))
    rw=[(a.shape[4],a.shape[5]) for a in arrs]
    D=go.shape[1]
    anys=pl.BlockSpec(memory_space=pl.ANY); vm=pl.BlockSpec(memory_space=pltpu.VMEM)
    scr=[V((Z,2,2)+s,bf) for s in rw]+[V((Z,2,2)+s,bf) for s in rw]+[V((Z,2)+s,bf) for s in rw]+[V((Z,)+s,bf) for s in rw[:3]]
    scr+=[V((Z,)+s,bf) for s in rw[:3]]+[V((Z,2)+rw[3],bf)]+[V(rw[3],bf)]*2
    scr+=[pltpu.SemaphoreType.DMA((4,Z)),pltpu.SemaphoreType.DMA((4,5,Z)),pltpu.SemaphoreType.DMA((4,5,Z))]
    return pl.pallas_call(functools.partial(reduce_kernel,Z),
        in_specs=[anys]*5,out_specs=[vm]*7+[anys],
        out_shape=tuple(sd(s,f32) for s in rw[:3])+tuple(sd((rw[2][0],D),f32) for _ in range(3))+(sd((rw[2][0],128),f32),sd(dxo.shape,bf)),
        scratch_shapes=scr,name="reduce_grads",
        cost_estimate=pl.CostEstimate(flops=10**7,bytes_accessed=30*2**20,transcendentals=0),
        compiler_params=pltpu.CompilerParams(vmem_limit_bytes=62*2**20,collective_id=1,has_side_effects=True))(*arrs,dxo)

from jax.sharding import PartitionSpec as P
ALL=("dp","mp")

XP=[(0,2),(2,0),(1,3),(3,1)]
CP=[(0,1),(1,0),(2,3),(3,2)]

def on_device(tokens, lengths, order, q_weight, k_weight, v_weight, o_weight, q_bias, v_bias, o_bias,
    attn_gain, attn_shift, in_weight, in_bias, out_weight, out_bias, ffn_gain, ffn_shift, cotangent):
    micro, rows, D = tokens.shape
    FF = in_weight.shape[1]
    G = lax.axis_size("dp")
    n = G*lax.axis_size("mp")
    g = lax.axis_index("dp"); m = lax.axis_index("mp")
    x = m//2; c = m%2
    sh = q_weight.shape[0]
    hw = D//2
    col = lambda v: v.reshape(sh,1)
    small = jnp.concatenate([col(v) for v in (q_bias,v_bias,o_bias,attn_gain,attn_shift,out_bias,ffn_gain,ffn_shift)]
        + [jnp.transpose(in_bias.reshape(FF//D,sh)), jnp.zeros((sh,128-8-FF//D),bf)],axis=1)
    qkv_l = jnp.concatenate([q_weight,k_weight,v_weight,small],axis=1)
    qkv = lax.all_gather(qkv_l,ALL,axis=0,tiled=True)
    oin = lax.all_gather(jnp.concatenate([o_weight,in_weight],axis=1),ALL,axis=0,tiled=True)
    w_out = lax.all_gather(out_weight,ALL,axis=0,tiled=True)
    w_o, w_in = oin[:,:D], oin[:,D:]
    smalls = jnp.transpose(qkv[:,3*D:])
    qb,vb,ob,ag,ash,outb,fg,fs = [smalls[i].astype(f32) for i in range(8)]
    inb = smalls[8:8+FF//D].reshape(FF//D,n,sh).transpose(1,0,2).reshape(FF).astype(f32)
    cut = lambda i: lax.dynamic_slice(qkv,(0,i*D+x*hw),(D,hw))
    wq,wk,wv = cut(0),cut(1),cut(2)
    wx = jnp.concatenate([wq,wk,wv],axis=1)
    xi = x.reshape(1).astype(jnp.int32)
    vec = jnp.stack([ob,ag,ash,outb,fg,fs,ob,ob])
    qbx = lax.dynamic_slice(qb,(x*hw,),(hw,)); vbx = lax.dynamic_slice(vb,(x*hw,),(hw,))
    R = rows//G
    mixed = lax.all_to_all(tokens.reshape(micro,G,R,D),"dp",split_axis=1,concat_axis=0,tiled=True).reshape(micro*G,R,D)
    picked = jnp.take(mixed,order,axis=0).reshape(G,micro,R,D)
    live_all = jnp.take(lengths,order,axis=0)
    outs=[];igs=[]
    st=[]
    for s in range(micro):
        own = lax.all_to_all(picked[:,s],"dp",split_axis=0,concat_axis=0,tiled=True).reshape(rows,D)
        oth = lax.ppermute(own,"mp",XP)
        X = jnp.concatenate([own,oth],axis=0)
        live = live_all[g*micro+s]
        sc = jnp.stack([live,c,x]).astype(jnp.int32)
        q = (jnp.dot(X,wq,preferred_element_type=f32)+qbx).astype(bf)
        k = jnp.dot(X,wk,preferred_element_type=f32).astype(bf)
        v = (jnp.dot(X,wv,preferred_element_type=f32)+vbx).astype(bf)
        kvo = jnp.concatenate([k,v],axis=1)
        kvs = lax.ppermute(kvo,"mp",CP)
        ctx,lse = attn_fwd(q,kvo,kvs,sc,rows)
        c_oth = lax.ppermute(ctx[rows:],"mp",XP)
        st.append([own,X,sc,q,kvo,kvs,ctx,lse,c_oth])
    own2 = jnp.stack([t[0] for t in st])
    cm = jnp.stack([t[6][:rows] for t in st]); co = jnp.stack([t[8] for t in st])
    out,dA,dck,dcs,gwo,gwin,gwout,gsm,ginb = ffn(xi,own2,cm,co,cotangent,w_o,w_in,w_out,vec,inb.reshape(1,FF))
    small_g = jnp.concatenate([jnp.zeros((2,D),f32),gsm[:6],ginb.reshape(n,FF//D,sh).transpose(1,0,2).reshape(FF//D,D),jnp.zeros((128-8-FF//D,D),f32)],axis=0)
    prev = jnp.zeros((D,3*hw+128),f32)
    igs=[]
    got = [lax.ppermute(dcs[s],"mp",XP) for s in range(micro)]
    for s in range(micro):
        own,X,sc,q,kvo,kvs,ctx,lse,c_oth = st[s]
        dctx = jnp.concatenate([dck[s],got[s]],axis=0)
        dq,dko,dvo,dks,dvs = attn_bwd(q,kvo,kvs,ctx,dctx,lse,sc,rows)
        r_ = lax.ppermute(jnp.concatenate([dks,dvs],axis=1),"mp",CP)
        last = s==micro-1
        ig,dxo,prev = qkvb(last,xi,X,dq,dko,dvo,r_,dA[s],wx,prev,small_g)
        igs.append((ig,dxo))
    rxa = lax.ppermute(igs[0][1],"mp",XP)
    gin,gout,go,gq,gk,gv,gs,rxb = reduce_grads(G,gwin,gwout,gwo,prev,igs[1][1])
    ig = jnp.stack([igs[0][0]+rxa.astype(f32),igs[1][0]+rxb.astype(f32)])
    sm = jnp.transpose(gs)
    ginb_o = sm[8:8+FF//D].reshape(-1)
    return (out,ig,gq,gk,gv,go,sm[0],sm[1],sm[2],sm[3],sm[4],gin,ginb_o,gout,sm[5],sm[6],sm[7])

def solution(mesh):
    r2=P(ALL,None); r1=P(ALL); t=P("dp","mp",None)
    return jax.shard_map(on_device,mesh=mesh,
        in_specs=(t,P(),P(),r2,r2,r2,r2,r1,r1,r1,r1,r1,r2,r1,r2,r1,r1,r1,t),
        out_specs=(t,t,r2,r2,r2,r2,r1,r1,r1,r1,r1,r2,r1,r2,r1,r1,r1),check_vma=False)
```
